128 devices in a mesh: fsdp: 8 (over y_lo, x), seq: 16 (over y_hi, z, core).
Axes of the slice: x: 4, y: 4 (y_hi: 2, y_lo: 2; y = y_hi * 2 + y_lo), z: 4, core: 2. Of those that a mesh axis runs over, the one named last changes fastest.
Arguments:
- inputs: bfloat16 [8, 2048, 1536], P('fsdp', 'seq'), may hold values from -6 to 6
- shift_scale: float32 [8, 2, 1536], P('fsdp'), may hold values from -3 to 3
- gate: float32 [8, 1536], P('fsdp'), may hold values from 0.5 to 1.5
- d_out: bfloat16 [8, 2048, 1536], P('fsdp', 'seq'), may hold values from -6 to 6
- w_qkv: bfloat16 [3, 1536, 1536], P(None, 'fsdp', 'seq'), may hold values from -0.15625 to 0.15625
- w_mlp_in: bfloat16 [1536, 6144], P('fsdp', 'seq'), may hold values from -0.15625 to 0.15625
- w_att_out: bfloat16 [1536, 1536], P('seq', 'fsdp'), may hold values from -0.0625 to 0.0625
- w_mlp_out: bfloat16 [6144, 1536], P('seq', 'fsdp'), may hold values from -0.0625 to 0.0625
- q_gain: float32 [96], replicated, may hold values from 0.1 to 1.9
- k_gain: float32 [96], replicated, may hold values from 0.1 to 1.9
Outputs:
- layer_out: bfloat16 [8, 2048, 1536], P('fsdp', 'seq')
- grad_input: bfloat16 [8, 2048, 1536], P('fsdp', 'seq')
- grad_qkv: float32 [3, 1536, 1536], P(None, 'fsdp', 'seq')
- grad_mlp_in: float32 [1536, 6144], P('fsdp', 'seq')
- grad_att_out: float32 [1536, 1536], P('seq', 'fsdp')
- grad_mlp_out: float32 [6144, 1536], P('seq', 'fsdp')
The draws below stay inside these ranges and needn't reach their ends.
All inputs are finite; a program needn't handle non-finite values.
Results may differ from the reference program's by a relative error of at most 0.013.
Values may be sent and summed in bfloat16 or wider, within the bound.
No kernel may reach another device: no remote copies, remote signals or barrier semaphores. Data moves between devices by JAX's collectives and lax.ppermute only.
A program may use at most 128 MiB of HBM per device.

```python
import math
import jax
import jax.numpy as jnp
from jax import lax

D = 1536
H = 16
HD = 96
FF = 6144
SEQ = 2048
BATCH = 8
N_SEQ = 16


def level_of(key, dims, cuts, low, largest):
    level = 1.0
    for dim, parts in cuts:
        draws = jax.random.uniform(jax.random.fold_in(jax.random.fold_in(key, 6), dim), (parts,), jnp.float32, low / len(cuts), largest / len(cuts))
        level = level * jnp.repeat(jnp.exp(draws), dims[dim] // parts).reshape((-1,) + (1,) * (len(dims) - 1 - dim))
    return level


def normal_values(own_key, shape, deviation, reach, pieces=(), kind=jnp.bfloat16):
    drawn = jax.random.normal(own_key, shape, jnp.float32) * deviation
    if len(pieces) > 0:
        drawn = level_of(own_key, shape, pieces, -0.22, 0.18) * drawn
    return jnp.clip(drawn, min=-reach, max=reach).astype(kind)


def setup_inputs(seed: int = 0) -> dict:
    keys = jax.random.split(jax.random.key(seed), 11)
    return {
        "inputs": normal_values(keys[0], (BATCH, SEQ, D), 1.0, 6.0, ((0, 8), (1, 16))),
        "shift_scale": normal_values(keys[1], (BATCH, 2, D), 0.5, 3.0, ((0, 8),), jnp.float32),
        "gate": jnp.clip(0.5 + 1.0 * jax.random.uniform(keys[2], (BATCH, D), jnp.float32) ** level_of(keys[2], (BATCH, D), ((0, 8),), -0.2, 0.2), 0.5, 1.5),
        "d_out": normal_values(keys[3], (BATCH, SEQ, D), 1.0, 6.0, ((0, 8), (1, 16))),
        "w_qkv": normal_values(keys[4], (3, D, H * HD), D ** -0.5, 0.15625, ((1, 8), (2, 16))),
        "w_mlp_in": normal_values(keys[5], (D, FF), D ** -0.5, 0.15625, ((0, 8), (1, 16))),
        "w_att_out": normal_values(keys[6], (H * HD, D), (H * HD + FF) ** -0.5, 0.0625, ((0, 16), (1, 8))),
        "w_mlp_out": normal_values(keys[7], (FF, D), (H * HD + FF) ** -0.5, 0.0625, ((0, 16), (1, 8))),
        "q_gain": jnp.clip(1.0 + 0.18 * jax.random.normal(keys[8], (HD,), jnp.float32), 0.1, 1.9),
        "k_gain": jnp.clip(1.0 + 0.18 * jax.random.normal(keys[9], (HD,), jnp.float32), 0.1, 1.9),
    }


def norm_heads(raw, gain):
    rows = raw.reshape(raw.shape[0], -1, gain.shape[0])
    inv = lax.rsqrt(lax.optimization_barrier(jnp.mean(rows * rows, axis=-1, keepdims=True)) + 1e-06)
    return (rows * inv * gain).reshape(raw.shape)

def gelu_tanh(values):
    return jax.nn.gelu(values, approximate=True)

def rounded(values):
    return lax.optimization_barrier(values.astype(jnp.bfloat16)).astype(jnp.float32)

def attend_forward(query, key, value, scale):
    scores = jnp.dot(query, key.T, preferred_element_type=jnp.float32) * scale
    expo = jnp.exp(scores)
    probs = (expo / lax.optimization_barrier(jnp.sum(expo, axis=-1, keepdims=True))).astype(jnp.bfloat16)
    return jnp.dot(probs, value, preferred_element_type=jnp.float32).astype(jnp.bfloat16)

def attend_backward(query, key, value, attended, d_att, scale):
    scores = jnp.dot(query, key.T, preferred_element_type=jnp.float32) * scale
    expo = jnp.exp(scores)
    weights = expo / lax.optimization_barrier(jnp.sum(expo, axis=-1, keepdims=True))
    probs = weights.astype(jnp.bfloat16)
    d_value = jnp.dot(probs.T, d_att, preferred_element_type=jnp.float32)
    d_probs = jnp.dot(d_att, value.T, preferred_element_type=jnp.float32)
    delta = lax.optimization_barrier(jnp.sum(d_att.astype(jnp.float32) * attended.astype(jnp.float32), axis=-1, keepdims=True))
    d_scores = (weights * (d_probs - delta)).astype(jnp.bfloat16)
    d_query = jnp.dot(d_scores, key, preferred_element_type=jnp.float32) * scale
    d_key = jnp.dot(d_scores.T, query, preferred_element_type=jnp.float32) * scale
    return (d_query, d_key, d_value.astype(jnp.bfloat16))

def reference(inputs, shift_scale, gate, d_out, w_qkv, w_mlp_in, w_att_out, w_mlp_out, q_gain, k_gain):
    scale = 1.0 / math.sqrt(HD)
    head_cols = H * HD // N_SEQ
    unit_cols = FF // N_SEQ
    groups = jnp.arange(N_SEQ, dtype=jnp.int32)

    def to_heads(values):
        return values.reshape(SEQ, H, HD).transpose(1, 0, 2)

    def from_heads(values):
        return values.transpose(1, 0, 2).reshape(SEQ, H * HD)

    def branch_sum(attended, hidden):

        def step(total, group):
            a_cols = lax.dynamic_slice_in_dim(attended, group * head_cols, head_cols, 1)
            a_rows = lax.dynamic_slice_in_dim(w_att_out, group * head_cols, head_cols, 0)
            h_cols = lax.dynamic_slice_in_dim(hidden, group * unit_cols, unit_cols, 1)
            h_rows = lax.dynamic_slice_in_dim(w_mlp_out, group * unit_cols, unit_cols, 0)
            part = jnp.dot(a_cols, a_rows, preferred_element_type=jnp.float32)
            part = part + jnp.dot(h_cols, h_rows, preferred_element_type=jnp.float32)
            return (total + rounded(part), None)
        total, _ = lax.scan(step, jnp.zeros((SEQ, D), jnp.float32), groups)
        return total

    def input_sum(d_raws, d_pre):

        def step(total, group):
            part = jnp.zeros((SEQ, D), jnp.float32)
            for index in range(3):
                d_cols = lax.dynamic_slice_in_dim(d_raws[index], group * head_cols, head_cols, 1)
                w_cols = lax.dynamic_slice_in_dim(w_qkv[index], group * head_cols, head_cols, 1)
                part = part + jnp.dot(d_cols, w_cols.T, preferred_element_type=jnp.float32)
            p_cols = lax.dynamic_slice_in_dim(d_pre, group * unit_cols, unit_cols, 1)
            m_cols = lax.dynamic_slice_in_dim(w_mlp_in, group * unit_cols, unit_cols, 1)
            part = part + jnp.dot(p_cols, m_cols.T, preferred_element_type=jnp.float32)
            return (total + rounded(part), None)
        total, _ = lax.scan(step, jnp.zeros((SEQ, D), jnp.float32), groups)
        return total

    def one_seq(carry, item):
        tokens, modul, gating, cotan = item
        xf = tokens.astype(jnp.float32)
        centered = xf - lax.optimization_barrier(jnp.mean(xf, axis=-1, keepdims=True))
        inv = lax.rsqrt(lax.optimization_barrier(jnp.mean(centered * centered, axis=-1, keepdims=True)) + 1e-06)
        normed = centered * inv
        modded = ((1.0 + modul[1]) * normed + modul[0]).astype(jnp.bfloat16)
        raw_q = jnp.dot(modded, w_qkv[0], preferred_element_type=jnp.float32)
        raw_k = jnp.dot(modded, w_qkv[1], preferred_element_type=jnp.float32)
        raw_v = jnp.dot(modded, w_qkv[2], preferred_element_type=jnp.float32)
        query = norm_heads(raw_q, q_gain).astype(jnp.bfloat16)
        key = norm_heads(raw_k, k_gain).astype(jnp.bfloat16)
        value = raw_v.astype(jnp.bfloat16)
        att_heads = lax.map(lambda t: attend_forward(t[0], t[1], t[2], scale), (to_heads(query), to_heads(key), to_heads(value)))
        attended = from_heads(att_heads)
        mlp_pre = jnp.dot(modded, w_mlp_in, preferred_element_type=jnp.float32)
        hidden = gelu_tanh(mlp_pre).astype(jnp.bfloat16)
        branch = branch_sum(attended, hidden)
        layer_out = (xf + gating * branch).astype(jnp.bfloat16)
        dyf = cotan.astype(jnp.float32)
        d_branch = (gating * dyf).astype(jnp.bfloat16)
        g_ao = jnp.dot(attended.T, d_branch, preferred_element_type=jnp.float32)
        g_mo = jnp.dot(hidden.T, d_branch, preferred_element_type=jnp.float32)
        d_att = jnp.dot(d_branch, w_att_out.T, preferred_element_type=jnp.float32).astype(jnp.bfloat16)
        d_hid = jnp.dot(d_branch, w_mlp_out.T, preferred_element_type=jnp.float32)
        _, pull_gelu = jax.vjp(gelu_tanh, mlp_pre)
        d_pre = pull_gelu(d_hid)[0].astype(jnp.bfloat16)
        dq_heads, dk_heads, dv_heads = lax.map(lambda t: attend_backward(t[0], t[1], t[2], t[3], t[4], scale), (to_heads(query), to_heads(key), to_heads(value), to_heads(attended), to_heads(d_att)))
        _, pull_q = jax.vjp(lambda t: norm_heads(t, q_gain), raw_q)
        _, pull_k = jax.vjp(lambda t: norm_heads(t, k_gain), raw_k)
        d_rq = pull_q(from_heads(dq_heads))[0].astype(jnp.bfloat16)
        d_rk = pull_k(from_heads(dk_heads))[0].astype(jnp.bfloat16)
        d_rv = from_heads(dv_heads)
        g_qkv = jnp.stack([jnp.dot(modded.T, d_rq, preferred_element_type=jnp.float32), jnp.dot(modded.T, d_rk, preferred_element_type=jnp.float32), jnp.dot(modded.T, d_rv, preferred_element_type=jnp.float32)])
        g_in = jnp.dot(modded.T, d_pre, preferred_element_type=jnp.float32)
        d_mod = input_sum((d_rq, d_rk, d_rv), d_pre)
        d_norm = (1.0 + modul[1]) * d_mod
        dx = dyf + inv * (d_norm - lax.optimization_barrier(jnp.mean(d_norm, axis=-1, keepdims=True)) - normed * lax.optimization_barrier(jnp.mean(d_norm * normed, axis=-1, keepdims=True)))
        new_carry = (carry[0] + rounded(g_qkv), carry[1] + rounded(g_in), carry[2] + rounded(g_ao), carry[3] + rounded(g_mo))
        return (new_carry, (layer_out, dx.astype(jnp.bfloat16)))
    init = (jnp.zeros((3, D, H * HD), jnp.float32), jnp.zeros((D, FF), jnp.float32), jnp.zeros((H * HD, D), jnp.float32), jnp.zeros((FF, D), jnp.float32))
    carry, (outs, grads_in) = lax.scan(one_seq, init, (inputs, shift_scale, gate, d_out))
    return (outs, grads_in, carry[0], carry[1], carry[2], carry[3])
```

```python
import functools
import math

import jax
import jax.numpy as jnp
from jax import lax
from jax.experimental import pallas as pl
from jax.experimental.pallas import tpu as pltpu
from jax.sharding import PartitionSpec as P


HD = 96
D = 1536
TOK = 128
SEQ = 2048
FFL = 384
PIECE = 192
WCOLS = 1152
QB = 256
KB = 512
SCALE = 1.0 / math.sqrt(HD)
LOG2E = 1.4426950408889634
LN2 = 0.6931471805599453
BF = jnp.bfloat16
F32 = jnp.float32
VMEM = pl.BlockSpec(memory_space=pltpu.VMEM)
ANY = pl.BlockSpec(memory_space=pl.ANY)
SMEM = pl.BlockSpec(memory_space=pltpu.SMEM)
LIMIT = 60 * 1024 * 1024


def call(kernel, outs, in_specs, scratch=(), flops=0, nbytes=0, out_specs=None, name=None):
    return pl.pallas_call(
        kernel,
        out_shape=outs,
        in_specs=in_specs,
        out_specs=out_specs if out_specs is not None else jax.tree.map(lambda _: VMEM, outs),
        scratch_shapes=list(scratch),
        compiler_params=pltpu.CompilerParams(vmem_limit_bytes=LIMIT),
        cost_estimate=pl.CostEstimate(flops=flops, bytes_accessed=nbytes, transcendentals=0),
        name=name,
    )


def sds(shape, dtype=BF):
    return jax.ShapeDtypeStruct(shape, dtype)


def dot(a, b):
    return jnp.dot(a, b, preferred_element_type=F32)


def dot_nt(a, b):
    return lax.dot_general(a, b, (((1,), (1,)), ((), ())), preferred_element_type=F32)


def dot_tn(a, b):
    return lax.dot_general(a, b, (((0,), (0,)), ((), ())), preferred_element_type=F32)


def seq_move(value, dy, dz, dc):
    pairs = []
    for src in range(16):
        y, z, c = src // 8, (src // 2) % 4, src % 2
        pairs.append((src, (y ^ dy) * 8 + ((z + dz) % 4) * 2 + (c ^ dc)))
    return lax.ppermute(value, "seq", pairs)


def fsdp_move(value, dy, dx):
    pairs = []
    for src in range(8):
        y, x = src // 4, src % 4
        pairs.append((src, (y ^ dy) * 4 + (x + dx) % 4))
    return lax.ppermute(value, "fsdp", pairs)


OFFSETS = ((0, 0), (1, 0), (0, -1), (0, 1), (1, -1), (1, 1), (0, 2), (1, 2))


def gather_ring(own, move):
    pair = move(own, 1, 0)
    left, right = move(own, 0, 1), move(own, 0, -1)
    left_p, right_p = move(pair, 0, 1), move(pair, 0, -1)
    far = move(left, 0, 1)
    far_p = move(right_p, 0, -1)
    return [own, pair, left, right, left_p, right_p, far, far_p]


def add_bf(*parts):
    total = parts[0].astype(F32)
    for part in parts[1:]:
        total = total + part.astype(F32)
    return total.astype(BF)


def scatter_ring(q, move):
    own, pair, left, right, left_p, right_p, far, far_p = q
    r1 = move(far, 0, 1)
    l1 = move(far_p, 0, -1)
    rp = move(right_p, 0, 1)
    lo = move(left, 0, -1)
    rr = move(add_bf(right, r1), 0, 1)
    ll = move(add_bf(left_p, l1), 0, -1)
    yy = move(add_bf(pair, rp, ll), 1, 0)
    return [own, lo, rr, yy]


def lane_iota(rows):
    return lax.broadcasted_iota(jnp.int32, (rows, 128), 1)


def pack_kernel(wqkv, win, wao, wmo, out):
    out[:, 0:FFL] = win[...]
    out[:, 384:480] = wqkv[0]
    out[:, 480:576] = wqkv[1]
    out[:, 576:672] = wqkv[2]
    out[:, 672:768] = wao[...].astype(F32).T.astype(BF)
    out[:, 768:1152] = wmo[...].astype(F32).T.astype(BF)


def normalize(xf):
    mean = jnp.mean(xf, axis=-1, keepdims=True)
    cen = xf - mean
    inv = lax.rsqrt(jnp.mean(cen * cen, axis=-1, keepdims=True) + 1e-6)
    return cen * inv, inv


def prologue_kernel(x, ss, gate, dout, modded, dbr):
    normed, _ = normalize(x[...].astype(F32))
    modded[...] = ((1.0 + ss[1:2, :]) * normed + ss[0:1, :]).astype(BF)
    dbr[...] = (gate[...] * dout[...].astype(F32)).astype(BF)


def project_kernel(offs, *refs):
    slots, pieces = refs[:16], refs[16:24]
    qg, kg = refs[24:26]
    w, qo, ko, vo, rq, rk, hid, gp = refs[26:34]
    feat, sems, wsems = refs[34:37]
    wcopies = []
    for i in range(8):
        at = pl.multiple_of(offs[i] * PIECE, PIECE)
        wcopies.append(pltpu.make_async_copy(pieces[i], w.at[pl.ds(at, PIECE)], wsems.at[i]))
        wcopies[-1].start()
    for i in range(16):
        pltpu.make_async_copy(slots[i], feat.at[pl.ds(i * TOK, TOK)], sems.at[i]).start()
    for cp in wcopies:
        cp.wait()
    lane = lane_iota(QB)

    def body(b, carry):
        for h in range(QB // TOK):
            i = b * (QB // TOK) + h
            pltpu.make_async_copy(
                slots[0], feat.at[pl.ds(pl.multiple_of(i * TOK, TOK), TOK)], sems.at[i]
            ).wait()
        rows = pl.ds(pl.multiple_of(b * QB, QB), QB)
        f = feat[rows, :]
        raw = dot(f, w[:, 384:768])
        t0, t1, t2 = raw[:, 0:128], raw[:, 128:256], raw[:, 256:384]
        live = lane < HD
        q = jnp.where(live, t0, 0.0)
        k = jnp.where(lane < 32, pltpu.roll(t0, 32, 1), pltpu.roll(t1, 32, 1))
        k = jnp.where(live, k, 0.0)
        v = jnp.where(lane < 64, pltpu.roll(t1, 64, 1), pltpu.roll(t2, 64, 1))
        v = jnp.where(live, v, jnp.where(lane < 98, 1.0, 0.0))
        vo[rows, :] = v.astype(BF)
        qi = lax.rsqrt(jnp.sum(q * q, axis=-1, keepdims=True) * (1.0 / HD) + 1e-6)
        ki = lax.rsqrt(jnp.sum(k * k, axis=-1, keepdims=True) * (1.0 / HD) + 1e-6)
        qh, kh = q * qi, k * ki
        qo[rows, :] = (qh * (qg[...] * (SCALE * LOG2E))).astype(BF)
        ko[rows, :] = (kh * kg[...]).astype(BF)
        rq[rows, :] = jnp.where(live, qh, qi)
        rk[rows, :] = jnp.where(live, kh, ki)
        pre = dot(f, w[:, 0:384])
        c0 = math.sqrt(2.0 / math.pi)
        sq = pre * pre
        t = jnp.tanh(c0 * (pre + 0.044715 * (sq * pre)))
        half = 0.5 * (1.0 + t)
        hid[rows, :] = (pre * half).astype(BF)
        gp[rows, :] = (
            half + (0.5 * c0) * pre * (1.0 - t * t) * (1.0 + (3.0 * 0.044715) * sq)
        ).astype(BF)
        return carry

    lax.fori_loop(0, SEQ // QB, body, 0)


def attention_kernel(*refs):
    slots = refs[:16]
    w, qi, ki, vi, rq, rk, hid, gp, qg, kg = refs[16:26]
    d1, a2 = refs[26:28]
    dbr, kt, vt, ebuf, dk, dv, sems = refs[28:35]
    for i in range(16):
        pltpu.make_async_copy(slots[i], dbr.at[pl.ds(i * TOK, TOK)], sems.at[i]).start()
    for j in range(SEQ // KB):
        cols = pl.ds(j * KB, KB)
        kt[:, cols] = ki[cols, :].astype(F32).T.astype(BF)
        vt[:, cols] = vi[cols, :].astype(F32).T.astype(BF)
    dk[...] = jnp.zeros_like(dk)
    dv[...] = jnp.zeros_like(dv)
    lane = lane_iota(QB)
    live = lane < HD
    row_id = lax.broadcasted_iota(jnp.int32, (128, QB), 0)

    def body(b, carry):
        for h in range(QB // TOK):
            i = b * (QB // TOK) + h
            pltpu.make_async_copy(
                slots[0], dbr.at[pl.ds(pl.multiple_of(i * TOK, TOK), TOK)], sems.at[i]
            ).wait()
        rows = pl.ds(pl.multiple_of(b * QB, QB), QB)
        dcat = dot(dbr[rows, :], w[:, 640:1152])
        d1[rows, 0:384] = (gp[rows, :].astype(F32) * dcat[:, 128:512]).astype(BF)
        da = jnp.where(live, pltpu.roll(dcat[:, 0:128], 96, 1), 0.0)
        do_t = da.T.astype(BF).astype(F32)
        qb = qi[rows, :]
        qt = qb.astype(F32).T.astype(BF)
        ot = jnp.zeros((128, QB), F32)
        for j in range(SEQ // KB):
            s = dot(ki[j * KB : (j + 1) * KB, :], qt)
            e = jnp.exp2(s).astype(BF)
            ebuf[j * KB : (j + 1) * KB, :] = e
            ot = ot + dot(vt[:, j * KB : (j + 1) * KB], e)
        linv = 1.0 / ot[96:97, :]
        att_t = jnp.where(row_id < HD, ot * linv, 0.0)
        att_r = att_t.astype(BF).astype(F32)
        delta = jnp.sum(do_t * att_r, axis=0, keepdims=True) * linv
        hi = delta.astype(BF).astype(F32)
        low = delta - hi
        dol_t = jnp.where(row_id < HD, do_t * linv, jnp.where(row_id == 96, -hi, -low))
        dol_t = jnp.where(row_id < 98, dol_t, 0.0)
        dol = dol_t.T.astype(BF)
        dol_t = dol_t.astype(BF)
        a2[rows, 0:128] = pltpu.roll(att_t.T, 32, 1).astype(BF)
        a2[rows, 128:512] = hid[rows, :]
        dqt = jnp.zeros((128, QB), F32)
        for j in range(SEQ // KB):
            kr = slice(j * KB, (j + 1) * KB)
            e = ebuf[kr, :]
            dp = dot(vi[kr, :], dol_t)
            ds = (e.astype(F32) * dp).astype(BF)
            dv[kr, :] = dv[kr, :] + dot(e, dol)
            dk[kr, :] = dk[kr, :] + dot(ds, qb)
            dqt = dqt + dot(kt[:, kr], ds)
        g = dqt.T * (qg[...] * SCALE)
        saved = rq[rows, :]
        hat = jnp.where(live, saved, 0.0)
        inv = saved[:, 96:97]
        dr = inv * (g - hat * (jnp.sum(g * hat, axis=-1, keepdims=True) * (1.0 / HD)))
        d1[rows, 384:512] = dr.astype(BF)
        return carry

    lax.fori_loop(0, SEQ // QB, body, 0)

    def tail(b, carry):
        rows = pl.ds(pl.multiple_of(b * QB, QB), QB)
        g = dk[rows, :] * (kg[...] * LN2)
        saved = rk[rows, :]
        hat = jnp.where(live, saved, 0.0)
        inv = saved[:, 96:97]
        dr = inv * (g - hat * (jnp.sum(g * hat, axis=-1, keepdims=True) * (1.0 / HD)))
        dr = pltpu.roll(jnp.where(live, dr, 0.0), 96, 1)
        vr = pltpu.roll(jnp.where(live, dv[rows, :], 0.0), 64, 1)
        q0 = d1[rows, 384:512].astype(F32)
        d1[rows, 384:512] = jnp.where(live, q0, dr).astype(BF)
        d1[rows, 512:640] = jnp.where(lane < 64, dr, vr).astype(BF)
        d1[rows, 640:768] = jnp.where(lane < 32, vr, 0.0).astype(BF)
        return carry

    lax.fori_loop(0, SEQ // QB, tail, 0)


def partial_first_kernel(lo, hi, a, w, out):
    def body(b, carry):
        rows = pl.ds(pl.multiple_of(b * QB, QB), QB)
        src = pl.ds(pl.multiple_of(b * QB + 1024, QB), QB)
        out[rows, :] = dot_nt(a[src, :], w[:, lo:hi]).astype(BF)
        return carry

    lax.fori_loop(0, 1024 // QB, body, 0)


def partial_second_kernel(lo, hi, a, w, recv, *outs):
    for b in range(8):
        rows = slice(b * TOK, (b + 1) * TOK)
        if b % 2 == 0:
            both = slice(b * TOK, (b + 2) * TOK)
            part = dot_nt(a[both, :], w[:, lo:hi]) + recv[both, :].astype(F32)
            outs[b][...] = part[:TOK].astype(BF)
            outs[b + 1][...] = part[TOK:].astype(BF)


def partial_sums(a, w, lo, hi):
    cols = hi - lo
    flops = 2 * 1024 * cols * D
    first = call(
        functools.partial(partial_first_kernel, lo, hi), sds((1024, D)), [VMEM] * 2,
        flops=flops, nbytes=8 << 20, name="partial_first",
    )(a, w)
    recv = seq_move(first, 0, 0, 1)
    blocks = call(
        functools.partial(partial_second_kernel, lo, hi), [sds((TOK, D))] * 8, [VMEM] * 3,
        flops=flops, nbytes=11 << 20, name="partial_second",
    )(a, w, recv)
    return scatter_ring(list(blocks), lambda v, dy, dz: seq_move(v, dy, dz, 0))


def grads_kernel(offs, *refs):
    slots, dslots = refs[:16], refs[16:32]
    d1, a2 = refs[32:34]
    outs = refs[34:42]
    feat, dbr, acc, sems, dsems = refs[42:47]
    for i in range(16):
        rows = pl.ds(i * TOK, TOK)
        pltpu.make_async_copy(dslots[i], dbr.at[rows], dsems.at[i]).start()
    for i in range(16):
        rows = pl.ds(i * TOK, TOK)
        pltpu.make_async_copy(slots[i], feat.at[rows], sems.at[i]).start()
    for i in range(16):
        rows = pl.ds(i * TOK, TOK)
        pltpu.make_async_copy(dslots[i], dbr.at[rows], dsems.at[i]).wait()
    for i in range(16):
        rows = pl.ds(i * TOK, TOK)
        pltpu.make_async_copy(slots[i], feat.at[rows], sems.at[i]).wait()

    def body(m, carry):
        cols = pl.ds(pl.multiple_of(m * 256, 256), 256)
        g2 = dot_tn(dbr[:, cols], a2[...])
        g1 = dot_tn(feat[:, cols], d1[...])
        acc[cols, 0:640] = g1[:, 0:640].astype(BF)
        acc[cols, 640:768] = (g1[:, 640:768] + g2[:, 0:128]).astype(BF)
        acc[cols, 768:1152] = g2[:, 128:512].astype(BF)
        return carry

    lax.fori_loop(0, D // 256, body, 0)
    for i in range(8):
        at = pl.multiple_of(offs[i] * PIECE, PIECE)
        outs[i][...] = acc[pl.ds(at, PIECE), :]


def total(parts):
    out = parts[0][...].astype(F32)
    for part in parts[1:]:
        out = out + part[...].astype(F32)
    return out


def out_kernel(x, gate, b0, b1, b2, b3, out):
    branch = total((b0, b1, b2, b3))
    out[...] = (x[...].astype(F32) + gate[...] * branch).astype(BF)


def input_grad_kernel(x, ss, dout, m0, m1, m2, m3, out):
    normed, inv = normalize(x[...].astype(F32))
    dn = (1.0 + ss[1:2, :]) * total((m0, m1, m2, m3))
    mean = jnp.mean(dn, axis=-1, keepdims=True)
    proj = jnp.mean(dn * normed, axis=-1, keepdims=True)
    out[...] = (dout[...].astype(F32) + inv * (dn - mean - normed * proj)).astype(BF)


def weight_out_kernel(g0, g1, g2, g3, gqkv, gin, gao, gmo):
    s = total((g0, g1, g2, g3))
    gin[...] = s[:, 0:384]
    gqkv[0] = s[:, 384:480]
    gqkv[1] = s[:, 480:576]
    gqkv[2] = s[:, 576:672]
    gao[...] = s[:, 672:768].T
    gmo[...] = s[:, 768:1152].T


def per_device(
    inputs, shift_scale, gate, d_out, w_qkv, w_mlp_in, w_att_out, w_mlp_out, q_gain, k_gain
):
    x, dout, ss = inputs[0], d_out[0], shift_scale[0]
    me = lax.axis_index("fsdp")
    ring, pair = me % 4, me // 4
    offs = jnp.stack([(pair ^ dy) * 4 + (ring + dx) % 4 for dy, dx in OFFSETS]).astype(jnp.int32)
    qg = jnp.pad(q_gain, (0, 128 - HD)).reshape(1, 128)
    kg = jnp.pad(k_gain, (0, 128 - HD)).reshape(1, 128)

    packed = call(
        pack_kernel, sds((PIECE, WCOLS)), [VMEM] * 4, nbytes=1 << 20, name="pack"
    )(w_qkv, w_mlp_in, w_att_out, w_mlp_out)
    modded, dbr = call(
        prologue_kernel, [sds((TOK, D))] * 2, [VMEM] * 4, nbytes=2 << 20, name="prologue"
    )(x, ss, gate, dout)
    pieces = gather_ring(packed, fsdp_move)
    seq_ring = lambda v, dy, dz: seq_move(v, dy, dz, 0)
    feats = gather_ring(modded, seq_ring)
    feats = feats + [seq_move(v, 0, 0, 1) for v in feats]
    dbrs = gather_ring(dbr, seq_ring)
    dbrs = dbrs + [seq_move(v, 0, 0, 1) for v in dbrs]

    w, q, k, v, rq, rk, hid, gp = call(
        project_kernel,
        [
            sds((D, WCOLS)), sds((SEQ, 128)), sds((SEQ, 128)), sds((SEQ, 128)),
            sds((SEQ, 128), F32), sds((SEQ, 128), F32), sds((SEQ, FFL)), sds((SEQ, FFL)),
        ],
        [SMEM] + [ANY] * 24 + [VMEM] * 2,
        scratch=[
            pltpu.VMEM((SEQ, D), BF),
            pltpu.SemaphoreType.DMA((16,)),
            pltpu.SemaphoreType.DMA((8,)),
        ],
        flops=2 * SEQ * D * 768, nbytes=16 << 20, name="project",
    )(offs, *feats, *pieces, qg, kg)

    d1, a2 = call(
        attention_kernel,
        [sds((SEQ, 768)), sds((SEQ, 512))],
        [ANY] * 16 + [VMEM] * 10,
        scratch=[
            pltpu.VMEM((SEQ, D), BF),
            pltpu.VMEM((128, SEQ), BF),
            pltpu.VMEM((128, SEQ), BF),
            pltpu.VMEM((SEQ, QB), BF),
            pltpu.VMEM((SEQ, 128), F32),
            pltpu.VMEM((SEQ, 128), F32),
            pltpu.SemaphoreType.DMA((16,)),
        ],
        flops=2 * SEQ * D * 512 + 12 * SEQ * SEQ * 256, nbytes=24 << 20, name="attention",
    )(*dbrs, w, q, k, v, rq, rk, hid, gp, qg, kg)

    branch = partial_sums(a2, w, 640, 1152)
    dmods = partial_sums(d1, w, 0, 768)
    gpieces = call(
        grads_kernel,
        [sds((PIECE, WCOLS))] * 8,
        [SMEM] + [ANY] * 32 + [VMEM] * 2,
        scratch=[
            pltpu.VMEM((SEQ, D), BF),
            pltpu.VMEM((SEQ, D), BF),
            pltpu.VMEM((D, WCOLS), BF),
            pltpu.SemaphoreType.DMA((16,)),
            pltpu.SemaphoreType.DMA((16,)),
        ],
        flops=2 * SEQ * D * 1280, nbytes=24 << 20, name="grads",
    )(offs, *feats, *dbrs, d1, a2)
    gterms = scatter_ring(list(gpieces), fsdp_move)

    layer_out = call(
        out_kernel, sds((TOK, D)), [VMEM] * 6, nbytes=3 << 20, name="layer_out"
    )(x, gate, *branch)
    d_in = call(
        input_grad_kernel, sds((TOK, D)), [VMEM] * 7, nbytes=3 << 20, name="input_grad"
    )(x, ss, dout, *dmods)
    grad_qkv, grad_in, grad_ao, grad_mo = call(
        weight_out_kernel,
        [
            sds((3, PIECE, HD), F32), sds((PIECE, FFL), F32),
            sds((HD, PIECE), F32), sds((FFL, PIECE), F32),
        ],
        [VMEM] * 4, nbytes=3 << 20, name="weight_out",
    )(*gterms)
    return (layer_out[None], d_in[None], grad_qkv, grad_in, grad_ao, grad_mo)


def solution(mesh):
    placed = (
        P("fsdp", "seq", None),
        P("fsdp", None, None),
        P("fsdp", None),
        P("fsdp", "seq", None),
        P(None, "fsdp", "seq"),
        P("fsdp", "seq"),
        P("seq", "fsdp"),
        P("seq", "fsdp"),
        P(),
        P(),
    )
    return jax.shard_map(
        per_device,
        mesh=mesh,
        in_specs=placed,
        out_specs=(
            P("fsdp", "seq", None),
            P("fsdp", "seq", None),
            P(None, "fsdp", "seq"),
            P("fsdp", "seq"),
            P("seq", "fsdp"),
            P("seq", "fsdp"),
        ),
        check_vma=False,
    )
```
